32 devices in a mesh: band: 8 (over z, x), quarter: 4 (over y, core).
Axes of the slice: x: 2, y: 2, z: 4, core: 2. Of those that a mesh axis runs over, the one named last changes fastest.
Arguments:
- voltages: bfloat16 [32, 2, 524288], P('band', None, 'quarter'), may hold values from -6 to 6
- flagged: int32 [32], P('band'), may hold values 0 or 1
- antenna_source_lookup: int32 [32], replicated, may hold values from 0 to 31, each once
Outputs:
- visibility: bfloat16 [2, 16, 64, 64], P(None, 'band', 'quarter')
The draws below stay inside these ranges and needn't reach their ends.
Inputs may be any that keep to these rules, and one draw needn't show every extreme that they name: `antenna_source_lookup`: every input antenna appears exactly once.
All inputs are finite; a program needn't handle non-finite values. No bound on the sum of `flagged` on one device may be relied on, other than what follows from the above.
Results may differ from the reference program's by a relative error of at most 0.0074.
Values may be sent and summed in bfloat16 or wider, within the bound.
A program may use at most 64 MiB of HBM per device.

```python
import math
import jax
import jax.numpy as jnp
from jax import lax

POLARIZATION_NUM = 2
FRAME = 8192
TAPS = 4
ANTENNA_COUNT = 32
SIG = 64
CHANNELS = 16
SPECTRA = 64
SIGNAL_SAMPLES = 524288


def touch_ends(entries, key, least, high):
    place = [jax.random.randint(jax.random.fold_in(key, axis), (), 0, length) for axis, length in enumerate(entries.shape)]
    widest = entries.shape.index(max(entries.shape))
    neighbour = place[:widest] + [(place[widest] + 1) % entries.shape[widest]] + place[widest + 1:]
    return entries.at[tuple(place)].set(least).at[tuple(neighbour)].set(high)


def shard_levels(stream_key, dims, cuts, least, top_value):
    def one(position, blocks):
        draws = jax.random.uniform(jax.random.fold_in(jax.random.fold_in(stream_key, 6), position), (blocks,), jnp.float32, least / len(cuts), top_value / len(cuts))
        return jnp.repeat(jnp.exp(draws), dims[position] // blocks).reshape((-1,) + (1,) * (len(dims) - position - 1))

    factor_of = one(*cuts[0])
    for cut in cuts[1:]:
        factor_of = factor_of * one(*cut)
    return factor_of


def normal_values(stream_key, extent, spread, most, pieces=(), kind=jnp.bfloat16):
    loudness = shard_levels(stream_key, extent, pieces, -0.22, 0.18) if pieces else 1.0
    result = jax.random.normal(stream_key, extent, jnp.float32) * spread * loudness
    return jnp.minimum(jnp.maximum(result, -most), most).astype(kind)


def setup_inputs(seed: int = 0) -> dict:
    key_list = jax.random.split(jax.random.key(seed), 4)
    voltages = normal_values(key_list[0], (ANTENNA_COUNT, POLARIZATION_NUM, SIGNAL_SAMPLES), 1.0, 6.0, ((0, 8), (2, 4)))
    flagged = touch_ends((jax.random.randint(key_list[1], (ANTENNA_COUNT,), 0, 8) < 1).astype(jnp.int32), jax.random.fold_in(key_list[1], 1), 0, 1)
    antenna_source_lookup = jax.random.permutation(key_list[2], ANTENNA_COUNT).astype(jnp.int32)
    return {"voltages": voltages, "flagged": flagged, "antenna_source_lookup": antenna_source_lookup}


def pfb_window():
    sample_pos = jnp.arange(TAPS * FRAME, dtype=jnp.float32) + 0.5
    offset_units = sample_pos / FRAME - TAPS / 2.0
    hann_taper = 0.5 - 0.5 * jnp.cos(sample_pos * (2.0 * math.pi / (TAPS * FRAME)))
    return (jnp.sinc(offset_units) * hann_taper).reshape(TAPS, FRAME)

def dft_rows(channels):
    bins = jnp.arange(channels, dtype=jnp.int32) + FRAME // 8
    sample_index = jnp.arange(FRAME, dtype=jnp.int32)
    phase_steps = bins[:, None] * sample_index[None, :] % FRAME
    angles = phase_steps.astype(jnp.float32) * (2.0 * math.pi / FRAME)
    stacked = jnp.stack([jnp.cos(angles), -jnp.sin(angles)], axis=1)
    return stacked.reshape(2 * channels, FRAME).astype(jnp.bfloat16)

def reference(voltages, flagged, antenna_source_lookup):
    window = pfb_window()
    dft_table = dft_rows(CHANNELS)
    keep_mask = (1 - flagged).astype(jnp.bfloat16)
    masked = voltages * keep_mask[:, None, None]
    inv_root = 1.0 / math.sqrt(FRAME)

    def one_antenna(signal_rows):
        padded = jnp.concatenate([signal_rows, jnp.zeros((POLARIZATION_NUM, (TAPS - 1) * FRAME), jnp.bfloat16)], axis=1)
        padded = padded.reshape(POLARIZATION_NUM, SPECTRA + TAPS - 1, FRAME)
        spectrum = jnp.zeros((2 * CHANNELS, POLARIZATION_NUM * SPECTRA), jnp.float32)
        for tap_index in range(TAPS):
            windowed = (window[tap_index] * padded[:, tap_index:tap_index + SPECTRA].astype(jnp.float32)).astype(jnp.bfloat16)
            windowed = windowed.reshape(POLARIZATION_NUM * SPECTRA, FRAME)
            spectrum = spectrum + lax.dot_general(dft_table, windowed, (((1,), (1,)), ((), ())), preferred_element_type=jnp.float32)
        spectrum = (spectrum * inv_root).astype(jnp.bfloat16)
        return spectrum.reshape(CHANNELS, 2, POLARIZATION_NUM, SPECTRA)
    spectra = lax.map(one_antenna, masked)
    ordered = jnp.take(spectra, antenna_source_lookup.astype(jnp.int32), axis=0)
    ordered = ordered.transpose(1, 2, 4, 0, 3).reshape(CHANNELS, 2, SPECTRA, SIG)

    def one_channel(channel_data):
        real_part = channel_data[0]
        imag_part = channel_data[1]
        left_real = jnp.concatenate([real_part, imag_part], axis=0)
        left_imag = jnp.concatenate([imag_part, -real_part], axis=0)
        real_sum = jnp.dot(left_real.T, left_real, preferred_element_type=jnp.float32)
        imag_sum = jnp.dot(left_imag.T, left_real, preferred_element_type=jnp.float32)
        product = jnp.stack([real_sum, imag_sum], axis=0) * (1.0 / SPECTRA)
        return product.astype(jnp.bfloat16)
    visibility = lax.map(one_channel, ordered)
    return visibility.transpose(1, 0, 2, 3)
```

```python
import functools
import math

import jax
import jax.numpy as jnp
import ml_dtypes
import numpy as np
from jax import lax
from jax.experimental import pallas as pl
from jax.experimental.pallas import tpu as pltpu
from jax.sharding import PartitionSpec as P

FRAME = 8192
TAPS = 4
CH_DEV = 2
LANES = 128
CHUNKS = 8
MESH = pl.DeviceIdType.MESH


def weights(bands):
    pos = np.arange(TAPS * FRAME) + 0.5
    window = np.sinc(pos / FRAME - TAPS / 2) * (0.5 - 0.5 * np.cos(2 * np.pi * pos / (TAPS * FRAME)))
    window = window.reshape(TAPS, FRAME)
    band = np.arange(bands)[None, :]
    channel = np.arange(CH_DEV)[:, None]
    bins = band * CH_DEV + channel + FRAME // 8
    phase = bins[:, :, None] * np.arange(FRAME) % FRAME
    angle = phase * (2 * np.pi / FRAME)
    table = np.stack([np.cos(angle), -np.sin(angle)], axis=1) / math.sqrt(FRAME)
    table = table.reshape(1, 2 * CH_DEV * bands, FRAME)
    both = (window[:, None, :] * table).reshape(TAPS * 2 * CH_DEV * bands, CHUNKS, FRAME // CHUNKS)
    return np.ascontiguousarray(both.transpose(1, 0, 2)).astype(ml_dtypes.bfloat16)


def kernel(bands, quarters, ants, pols, spec, flag_ref, look_ref, x_ref, w_ref, out_ref,
           xb, wb, xf, sf, send, recv, rf, x_sem, w_sem, own_sem, send_sem, recv_sem):
    count = bands * quarters
    parts = 2 * CH_DEV
    my_band, my_quarter = lax.axis_index("band"), lax.axis_index("quarter")
    me = my_quarter * bands + my_band
    wide = xb.shape[2] // pols

    def x_copy(g):
        return pltpu.make_async_copy(x_ref.at[:, pl.ds(g * pols * wide, pols * wide), :], xb.at[g], x_sem.at[g])

    def w_copy(g):
        return pltpu.make_async_copy(w_ref.at[g], wb.at[g], w_sem.at[g])

    for g in range(CHUNKS):
        x_copy(g).start()
        w_copy(g).start()

    barrier = pltpu.get_barrier_semaphore()

    def device(k):
        d = lax.rem(me + k, count)
        return d, lax.rem(d, bands), lax.div(d, bands)

    @pl.loop(1, count)
    def _(k):
        _, b, q = device(k)
        pl.semaphore_signal(barrier, inc=1, device_id=(b, q), device_id_type=MESH)

    acc = None
    rows = x_ref.shape[0]
    for g in range(CHUNKS):
        x_copy(g).wait()
        w_copy(g).wait()
        xf[...] = xb[g].astype(jnp.float32).reshape(rows * pols * wide, LANES)
        pieces = []
        for j in range(wide):
            pieces.append(jnp.concatenate(
                [xf[pl.ds(pols * j + p, rows, stride=pols * wide), :] for p in range(pols)], axis=0
            ).astype(jnp.bfloat16))
        block = jnp.concatenate(pieces, axis=1)
        part = lax.dot_general(wb[g], block, (((1,), (1,)), ((), ())), preferred_element_type=jnp.float32)
        acc = part if acc is None else acc + part

    group = parts * bands
    columns = pols * rows
    lane = lax.broadcasted_iota(jnp.int32, (1, columns), 1)
    spot = lane % spec
    ant = (lane // spec) % ants
    keep = jnp.zeros((1, columns), jnp.float32)
    for a in range(ants):
        keep = jnp.where(ant == a, (1 - flag_ref[a]).astype(jnp.float32), keep)
    main = acc[:group]
    halo = jnp.zeros_like(main)
    for t in range(1, TAPS):
        moved = pltpu.roll(acc[t * group:(t + 1) * group], columns - t, 1)
        inside = spot + t < spec
        main = main + jnp.where(inside, moved, 0.0)
        halo = halo + jnp.where(inside, 0.0, moved)
    main = main * keep
    halo = pltpu.roll(halo, spec, 1) * keep
    for k in range(parts):
        sf[pl.ds(k, bands, stride=2 * parts), :] = main[k * bands:(k + 1) * bands]
        sf[pl.ds(parts + k, bands, stride=2 * parts), :] = halo[k * bands:(k + 1) * bands]
    send[...] = sf[...].reshape(bands, 2 * parts, columns).astype(jnp.bfloat16)

    pl.semaphore_wait(barrier, count - 1)

    def remote(k):
        _, b, q = device(k)
        return pltpu.make_async_remote_copy(
            src_ref=send.at[b], dst_ref=recv.at[me], send_sem=send_sem.at[k], recv_sem=recv_sem.at[me],
            device_id=(b, q), device_id_type=MESH)

    @pl.loop(1, count)
    def _(k):
        remote(k).start()

    own = pltpu.make_async_copy(send.at[my_band], recv.at[me], own_sem)
    own.start()

    signals = bands * ants * pols
    antennas = bands * ants
    look = look_ref[...].astype(jnp.float32)
    out_rows = signals // quarters

    def chooser(first, size):
        g = first + lax.broadcasted_iota(jnp.int32, (size, antennas), 0)
        i = lax.broadcasted_iota(jnp.int32, (size, antennas), 1)
        source = jnp.sum(jnp.where(i == g // pols, look, 0.0), axis=1, keepdims=True)
        g = first + lax.broadcasted_iota(jnp.int32, (size, signals), 0)
        row = lax.broadcasted_iota(jnp.int32, (size, signals), 1)
        kind = row // bands
        antenna = ((row % bands) * ants + kind % ants).astype(jnp.float32)
        hit = jnp.logical_and(antenna == source, g % pols == kind // ants)
        return jnp.where(hit, 1.0, 0.0).astype(jnp.bfloat16)

    all_rows = chooser(0, signals)
    own_rows = chooser(my_quarter * out_rows, out_rows)

    own.wait()

    @pl.loop(1, count)
    def _(k):
        remote(k).wait_send()
        d, b, q = device(k)
        pltpu.make_async_remote_copy(
            src_ref=send.at[b], dst_ref=recv.at[d], send_sem=send_sem.at[k], recv_sem=recv_sem.at[d],
            device_id=(b, q), device_id_type=MESH).wait_recv()

    rf[...] = recv[...].astype(jnp.float32).reshape(count * 2 * parts, columns)

    def rows_of(q, k):
        return rf[pl.ds(q * bands * 2 * parts + k, bands, stride=2 * parts), :]

    flipped = lax.broadcasted_iota(jnp.int32, (1, columns), 1)
    scale = 1.0 / (spec * quarters)
    for c in range(CH_DEV):
        blocks = []
        for r in range(2):
            for q in range(quarters):
                full = rows_of(q, 2 * c + r)
                if q + 1 < quarters:
                    full = full + rows_of(q + 1, parts + 2 * c + r)
                blocks.append(full.astype(jnp.bfloat16).astype(jnp.float32))
        bands_of = []
        for s in range(ants * pols):
            turned = None
            for at, block in enumerate(blocks):
                by = (spec * (at - s)) % columns
                moved = pltpu.roll(block, by, 1) if by else block
                turned = moved if turned is None else jnp.where(lane // spec == at, moved, turned)
            bands_of.append(turned)
        got = jnp.concatenate(bands_of, axis=0).astype(jnp.bfloat16)
        right = jnp.dot(all_rows, got, preferred_element_type=jnp.float32).astype(jnp.bfloat16)
        left = jnp.dot(own_rows, got, preferred_element_type=jnp.float32)
        other = pltpu.roll(left, columns // 2, 1)
        other = jnp.where(flipped < columns // 2, other, -other).astype(jnp.bfloat16)
        for o, side in enumerate((left.astype(jnp.bfloat16), other)):
            product = lax.dot_general(side, right, (((1,), (1,)), ((), ())), preferred_element_type=jnp.float32)
            out_ref[o, c] = (product * scale).astype(jnp.bfloat16)


def shards(table, bands, quarters, voltages, flagged, lookup):
    ants, pols, samples = voltages.shape
    spec = samples // FRAME
    steps = FRAME // LANES
    rows = ants * spec
    columns = pols * rows
    x = voltages.reshape(ants, pols, samples // LANES, LANES).transpose(0, 2, 1, 3).reshape(rows, steps * pols, LANES)
    signals = bands * ants * pols
    parts = 2 * CH_DEV
    count = bands * quarters
    group = TAPS * parts * bands
    return pl.pallas_call(
        functools.partial(kernel, bands, quarters, ants, pols, spec),
        out_shape=jax.ShapeDtypeStruct((2, CH_DEV, signals // quarters, signals), jnp.bfloat16),
        in_specs=[
            pl.BlockSpec(memory_space=pltpu.SMEM),
            pl.BlockSpec(memory_space=pltpu.VMEM),
            pl.BlockSpec(memory_space=pl.ANY),
            pl.BlockSpec(memory_space=pl.ANY),
        ],
        out_specs=pl.BlockSpec(memory_space=pltpu.VMEM),
        scratch_shapes=[
            pltpu.VMEM((CHUNKS, rows, steps * pols // CHUNKS, LANES), jnp.bfloat16),
            pltpu.VMEM((CHUNKS, group, FRAME // CHUNKS), jnp.bfloat16),
            pltpu.VMEM((rows * steps * pols // CHUNKS, LANES), jnp.float32),
            pltpu.VMEM((bands * 2 * parts, columns), jnp.float32),
            pltpu.VMEM((bands, 2 * parts, columns), jnp.bfloat16),
            pltpu.VMEM((count, 2 * parts, columns), jnp.bfloat16),
            pltpu.VMEM((count * 2 * parts, columns), jnp.float32),
            pltpu.SemaphoreType.DMA((CHUNKS,)),
            pltpu.SemaphoreType.DMA((CHUNKS,)),
            pltpu.SemaphoreType.DMA,
            pltpu.SemaphoreType.DMA((count,)),
            pltpu.SemaphoreType.DMA((count,)),
        ],
        compiler_params=pltpu.CompilerParams(
            collective_id=0, has_side_effects=True, vmem_limit_bytes=63 * 1024 * 1024),
    )(flagged, lookup.reshape(1, -1), x, jnp.asarray(table))


def solution(mesh):
    bands, quarters = mesh.shape["band"], mesh.shape["quarter"]
    return jax.shard_map(
        functools.partial(shards, weights(bands), bands, quarters),
        mesh=mesh,
        in_specs=(P("band", None, "quarter"), P("band"), P()),
        out_specs=P(None, "band", "quarter", None),
        check_vma=False,
    )
```

```python
import functools
import math

import jax
import jax.numpy as jnp
import ml_dtypes
import numpy as np
from jax import lax
from jax.experimental import pallas as pl
from jax.experimental.pallas import tpu as pltpu
from jax.sharding import PartitionSpec as P

FRAME = 8192
TAPS = 4
CH_DEV = 2
LANES = 128
CHUNKS = 8
MESH = pl.DeviceIdType.MESH


def weights(bands):
    pos = np.arange(TAPS * FRAME) + 0.5
    window = np.sinc(pos / FRAME - TAPS / 2) * (0.5 - 0.5 * np.cos(2 * np.pi * pos / (TAPS * FRAME)))
    window = window.reshape(TAPS, FRAME)
    band = np.arange(bands)[None, :]
    channel = np.arange(CH_DEV)[:, None]
    bins = band * CH_DEV + channel + FRAME // 8
    phase = bins[:, :, None] * np.arange(FRAME) % FRAME
    angle = phase * (2 * np.pi / FRAME)
    table = np.stack([np.cos(angle), -np.sin(angle)], axis=1) / math.sqrt(FRAME)
    table = table.reshape(1, 2 * CH_DEV * bands, FRAME)
    both = (window[:, None, :] * table).reshape(TAPS * 2 * CH_DEV * bands, CHUNKS, FRAME // CHUNKS)
    return np.ascontiguousarray(both.transpose(1, 0, 2)).astype(ml_dtypes.bfloat16)


def kernel(bands, quarters, ants, pols, spec, flag_in, look_in, x_ref, w_ref, out_ref,
           flag_ref, look_ref, xb, wb, xf, sf, send, recv, rf, x_sem, w_sem, flag_sem, look_sem, own_sem, send_sem, recv_sem):
    count = bands * quarters
    parts = 2 * CH_DEV
    my_band, my_quarter = lax.axis_index("band"), lax.axis_index("quarter")
    me = my_quarter * bands + my_band
    wide = xb.shape[2] // pols

    def x_copy(g):
        return pltpu.make_async_copy(x_ref.at[:, pl.ds(g * pols * wide, pols * wide), :], xb.at[g], x_sem.at[g])

    def w_copy(g):
        return pltpu.make_async_copy(w_ref.at[g], wb.at[g], w_sem.at[g])

    for g in range(CHUNKS):
        x_copy(g).start()
        w_copy(g).start()

    flag_copy = pltpu.make_async_copy(flag_in, flag_ref, flag_sem)
    look_copy = pltpu.make_async_copy(look_in, look_ref, look_sem)
    flag_copy.start()
    look_copy.start()

    barrier = pltpu.get_barrier_semaphore()

    def device(k):
        d = lax.rem(me + k, count)
        return d, lax.rem(d, bands), lax.div(d, bands)

    @pl.loop(1, count)
    def _(k):
        _, b, q = device(k)
        pl.semaphore_signal(barrier, inc=1, device_id=(b, q), device_id_type=MESH)

    acc = None
    rows = x_ref.shape[0]
    for g in range(CHUNKS):
        x_copy(g).wait()
        w_copy(g).wait()
        xf[...] = xb[g].astype(jnp.float32).reshape(rows * pols * wide, LANES)
        pieces = []
        for j in range(wide):
            pieces.append(jnp.concatenate(
                [xf[pl.ds(pols * j + p, rows, stride=pols * wide), :] for p in range(pols)], axis=0
            ).astype(jnp.bfloat16))
        block = jnp.concatenate(pieces, axis=1)
        part = lax.dot_general(wb[g], block, (((1,), (1,)), ((), ())), preferred_element_type=jnp.float32)
        acc = part if acc is None else acc + part

    group = parts * bands
    columns = pols * rows
    lane = lax.broadcasted_iota(jnp.int32, (1, columns), 1)
    spot = lane % spec
    ant = (lane // spec) % ants
    flag_copy.wait()
    keep = jnp.zeros((1, columns), jnp.float32)
    for a in range(ants):
        keep = jnp.where(ant == a, (1 - flag_ref[a]).astype(jnp.float32), keep)
    main = acc[:group]
    halo = jnp.zeros_like(main)
    for t in range(1, TAPS):
        moved = pltpu.roll(acc[t * group:(t + 1) * group], columns - t, 1)
        inside = spot + t < spec
        main = main + jnp.where(inside, moved, 0.0)
        halo = halo + jnp.where(inside, 0.0, moved)
    main = main * keep
    halo = pltpu.roll(halo, spec, 1) * keep
    for k in range(parts):
        sf[pl.ds(k, bands, stride=2 * parts), :] = main[k * bands:(k + 1) * bands]
        sf[pl.ds(parts + k, bands, stride=2 * parts), :] = halo[k * bands:(k + 1) * bands]
    send[...] = sf[...].reshape(bands, 2 * parts, columns).astype(jnp.bfloat16)

    pl.semaphore_wait(barrier, count - 1)

    def remote(k):
        _, b, q = device(k)
        return pltpu.make_async_remote_copy(
            src_ref=send.at[b], dst_ref=recv.at[me], send_sem=send_sem.at[k], recv_sem=recv_sem.at[me],
            device_id=(b, q), device_id_type=MESH)

    @pl.loop(1, count)
    def _(k):
        remote(k).start()

    own = pltpu.make_async_copy(send.at[my_band], recv.at[me], own_sem)
    own.start()

    signals = bands * ants * pols
    antennas = bands * ants
    look_copy.wait()
    look = look_ref[...].astype(jnp.float32)
    out_rows = signals // quarters

    def chooser(first, size):
        g = first + lax.broadcasted_iota(jnp.int32, (size, antennas), 0)
        i = lax.broadcasted_iota(jnp.int32, (size, antennas), 1)
        source = jnp.sum(jnp.where(i == g // pols, look, 0.0), axis=1, keepdims=True)
        g = first + lax.broadcasted_iota(jnp.int32, (size, signals), 0)
        row = lax.broadcasted_iota(jnp.int32, (size, signals), 1)
        kind = row // bands
        antenna = ((row % bands) * ants + kind % ants).astype(jnp.float32)
        hit = jnp.logical_and(antenna == source, g % pols == kind // ants)
        return jnp.where(hit, 1.0, 0.0).astype(jnp.bfloat16)

    all_rows = chooser(0, signals)
    own_rows = chooser(my_quarter * out_rows, out_rows)

    own.wait()

    @pl.loop(1, count)
    def _(k):
        remote(k).wait_send()
        d, b, q = device(k)
        pltpu.make_async_remote_copy(
            src_ref=send.at[b], dst_ref=recv.at[d], send_sem=send_sem.at[k], recv_sem=recv_sem.at[d],
            device_id=(b, q), device_id_type=MESH).wait_recv()

    rf[...] = recv[...].astype(jnp.float32).reshape(count * 2 * parts, columns)

    def rows_of(q, k):
        return rf[pl.ds(q * bands * 2 * parts + k, bands, stride=2 * parts), :]

    flipped = lax.broadcasted_iota(jnp.int32, (1, columns), 1)
    scale = 1.0 / (spec * quarters)
    for c in range(CH_DEV):
        blocks = []
        for r in range(2):
            for q in range(quarters):
                full = rows_of(q, 2 * c + r)
                if q + 1 < quarters:
                    full = full + rows_of(q + 1, parts + 2 * c + r)
                blocks.append(full.astype(jnp.bfloat16).astype(jnp.float32))
        bands_of = []
        for s in range(ants * pols):
            turned = None
            for at, block in enumerate(blocks):
                by = (spec * (at - s)) % columns
                moved = pltpu.roll(block, by, 1) if by else block
                turned = moved if turned is None else jnp.where(lane // spec == at, moved, turned)
            bands_of.append(turned)
        got = jnp.concatenate(bands_of, axis=0).astype(jnp.bfloat16)
        right = jnp.dot(all_rows, got, preferred_element_type=jnp.float32).astype(jnp.bfloat16)
        left = jnp.dot(own_rows, got, preferred_element_type=jnp.float32)
        other = pltpu.roll(left, columns // 2, 1)
        other = jnp.where(flipped < columns // 2, other, -other).astype(jnp.bfloat16)
        for o, side in enumerate((left.astype(jnp.bfloat16), other)):
            product = lax.dot_general(side, right, (((1,), (1,)), ((), ())), preferred_element_type=jnp.float32)
            out_ref[o, c] = (product * scale).astype(jnp.bfloat16)


def shards(table, bands, quarters, voltages, flagged, lookup):
    ants, pols, samples = voltages.shape
    spec = samples // FRAME
    steps = FRAME // LANES
    rows = ants * spec
    columns = pols * rows
    x = voltages.reshape(ants, pols, samples // LANES, LANES).transpose(0, 2, 1, 3).reshape(rows, steps * pols, LANES)
    signals = bands * ants * pols
    parts = 2 * CH_DEV
    count = bands * quarters
    group = TAPS * parts * bands
    room = 2 * table.size + 8 * columns * FRAME + 24 * count * parts * columns + 16 * 1024 * 1024
    return pl.pallas_call(
        functools.partial(kernel, bands, quarters, ants, pols, spec),
        out_shape=jax.ShapeDtypeStruct((2, CH_DEV, signals // quarters, signals), jnp.bfloat16),
        in_specs=[
            pl.BlockSpec(memory_space=pltpu.HBM),
            pl.BlockSpec(memory_space=pltpu.HBM),
            pl.BlockSpec(memory_space=pltpu.HBM),
            pl.BlockSpec(memory_space=pltpu.HBM),
        ],
        out_specs=pl.BlockSpec(memory_space=pltpu.VMEM),
        scratch_shapes=[
            pltpu.SMEM((ants,), jnp.int32),
            pltpu.VMEM((1, bands * ants), jnp.int32),
            pltpu.VMEM((CHUNKS, rows, steps * pols // CHUNKS, LANES), jnp.bfloat16),
            pltpu.VMEM((CHUNKS, group, FRAME // CHUNKS), jnp.bfloat16),
            pltpu.VMEM((rows * steps * pols // CHUNKS, LANES), jnp.float32),
            pltpu.VMEM((bands * 2 * parts, columns), jnp.float32),
            pltpu.VMEM((bands, 2 * parts, columns), jnp.bfloat16),
            pltpu.VMEM((count, 2 * parts, columns), jnp.bfloat16),
            pltpu.VMEM((count * 2 * parts, columns), jnp.float32),
            pltpu.SemaphoreType.DMA((CHUNKS,)),
            pltpu.SemaphoreType.DMA((CHUNKS,)),
            pltpu.SemaphoreType.DMA,
            pltpu.SemaphoreType.DMA,
            pltpu.SemaphoreType.DMA,
            pltpu.SemaphoreType.DMA((count,)),
            pltpu.SemaphoreType.DMA((count,)),
        ],
        compiler_params=pltpu.CompilerParams(
            collective_id=0, has_side_effects=True, vmem_limit_bytes=min(room, 63 * 1024 * 1024)),
    )(*[pltpu.with_memory_space_constraint(v, pltpu.HBM) for v in (flagged, lookup.reshape(1, -1), x, jnp.asarray(table))])


def solution(mesh):
    bands, quarters = mesh.shape["band"], mesh.shape["quarter"]
    return jax.shard_map(
        functools.partial(shards, weights(bands), bands, quarters),
        mesh=mesh,
        in_specs=(P("band", None, "quarter"), P("band"), P()),
        out_specs=P(None, "band", "quarter", None),
        check_vma=False,
    )
```

```python
import functools
import math

import jax
import jax.numpy as jnp
import ml_dtypes
import numpy as np
from jax import lax
from jax.experimental import pallas as pl
from jax.experimental.pallas import tpu as pltpu
from jax.sharding import PartitionSpec as P

FRAME = 8192
TAPS = 4
CH_DEV = 2
LANES = 128
CHUNKS = 8
MESH = pl.DeviceIdType.MESH


def weights(bands):
    pos = np.arange(TAPS * FRAME) + 0.5
    window = np.sinc(pos / FRAME - TAPS / 2) * (0.5 - 0.5 * np.cos(2 * np.pi * pos / (TAPS * FRAME)))
    window = window.reshape(TAPS, FRAME)
    band = np.arange(bands)[None, :]
    channel = np.arange(CH_DEV)[:, None]
    bins = band * CH_DEV + channel + FRAME // 8
    phase = bins[:, :, None] * np.arange(FRAME) % FRAME
    angle = phase * (2 * np.pi / FRAME)
    table = np.stack([np.cos(angle), -np.sin(angle)], axis=1) / math.sqrt(FRAME)
    table = table.reshape(1, 2 * CH_DEV * bands, FRAME)
    both = (window[:, None, :] * table).reshape(TAPS * 2 * CH_DEV * bands, CHUNKS, FRAME // CHUNKS)
    return np.ascontiguousarray(both.transpose(1, 0, 2)).astype(ml_dtypes.bfloat16)


def kernel(bands, quarters, ants, pols, spec, flag_in, look_in, x_ref, w_ref, out_ref,
           flag_ref, look_ref, xb, wb, xf, sf, send, recv, rf, x_sem, w_sem, flag_sem, look_sem, own_sem, send_sem, recv_sem):
    count = bands * quarters
    parts = 2 * CH_DEV
    my_band, my_quarter = lax.axis_index("band"), lax.axis_index("quarter")
    me = my_quarter * bands + my_band
    wide = xb.shape[2] // pols

    def x_copy(g):
        return pltpu.make_async_copy(x_ref.at[:, pl.ds(g * pols * wide, pols * wide), :], xb.at[g], x_sem.at[g])

    def w_copy(g):
        return pltpu.make_async_copy(w_ref.at[g], wb.at[g], w_sem.at[g])

    for g in range(CHUNKS):
        x_copy(g).start()
        w_copy(g).start()

    flag_copy = pltpu.make_async_copy(flag_in, flag_ref, flag_sem)
    look_copy = pltpu.make_async_copy(look_in, look_ref, look_sem)
    flag_copy.start()
    look_copy.start()

    barrier = pltpu.get_barrier_semaphore()

    def device(k):
        d = lax.rem(me + k, count)
        return d, lax.rem(d, bands), lax.div(d, bands)

    @pl.loop(1, count)
    def _(k):
        _, b, q = device(k)
        pl.semaphore_signal(barrier, inc=1, device_id=(b, q), device_id_type=MESH)

    acc = None
    rows = x_ref.shape[0]
    for g in range(CHUNKS):
        x_copy(g).wait()
        w_copy(g).wait()
        spread = pols * wide + 8
        for row in range(rows):
            xf[row * spread:row * spread + pols * wide, :] = xb[g, row].astype(jnp.float32)
        pieces = []
        for j in range(wide):
            pieces.append(jnp.concatenate(
                [xf[pl.ds(pols * j + p, rows, stride=spread), :] for p in range(pols)], axis=0
            ).astype(jnp.bfloat16))
        block = jnp.concatenate(pieces, axis=1)
        part = lax.dot_general(wb[g], block, (((1,), (1,)), ((), ())), preferred_element_type=jnp.float32)
        acc = part if acc is None else acc + part

    group = parts * bands
    columns = pols * rows
    lane = lax.broadcasted_iota(jnp.int32, (1, columns), 1)
    spot = lane % spec
    ant = (lane // spec) % ants
    flag_copy.wait()
    keep = jnp.zeros((1, columns), jnp.float32)
    for a in range(ants):
        keep = jnp.where(ant == a, (1 - flag_ref[a]).astype(jnp.float32), keep)
    main = acc[:group]
    halo = jnp.zeros_like(main)
    for t in range(1, TAPS):
        moved = pltpu.roll(acc[t * group:(t + 1) * group], columns - t, 1)
        inside = spot + t < spec
        main = main + jnp.where(inside, moved, 0.0)
        halo = halo + jnp.where(inside, 0.0, moved)
    main = main * keep
    halo = pltpu.roll(halo, spec, 1) * keep
    for k in range(parts):
        sf[pl.ds(k, bands, stride=2 * parts), :] = main[k * bands:(k + 1) * bands]
        sf[pl.ds(parts + k, bands, stride=2 * parts), :] = halo[k * bands:(k + 1) * bands]
    send[...] = sf[...].reshape(bands, 2 * parts, columns).astype(jnp.bfloat16)

    pl.semaphore_wait(barrier, count - 1)

    def remote(k):
        _, b, q = device(k)
        return pltpu.make_async_remote_copy(
            src_ref=send.at[b], dst_ref=recv.at[me], send_sem=send_sem.at[k], recv_sem=recv_sem.at[me],
            device_id=(b, q), device_id_type=MESH)

    @pl.loop(1, count)
    def _(k):
        remote(k).start()

    own = pltpu.make_async_copy(send.at[my_band], recv.at[me], own_sem)
    own.start()

    signals = bands * ants * pols
    antennas = bands * ants
    look_copy.wait()
    look = look_ref[...].astype(jnp.float32)
    out_rows = signals // quarters

    def chooser(first, size):
        g = first + lax.broadcasted_iota(jnp.int32, (size, antennas), 0)
        i = lax.broadcasted_iota(jnp.int32, (size, antennas), 1)
        source = jnp.sum(jnp.where(i == g // pols, look, 0.0), axis=1, keepdims=True)
        g = first + lax.broadcasted_iota(jnp.int32, (size, signals), 0)
        row = lax.broadcasted_iota(jnp.int32, (size, signals), 1)
        kind = row // bands
        antenna = ((row % bands) * ants + kind % ants).astype(jnp.float32)
        hit = jnp.logical_and(antenna == source, g % pols == kind // ants)
        return jnp.where(hit, 1.0, 0.0).astype(jnp.bfloat16)

    all_rows = chooser(0, signals)
    own_rows = chooser(my_quarter * out_rows, out_rows)

    own.wait()

    @pl.loop(1, count)
    def _(k):
        remote(k).wait_send()
        d, b, q = device(k)
        pltpu.make_async_remote_copy(
            src_ref=send.at[b], dst_ref=recv.at[d], send_sem=send_sem.at[k], recv_sem=recv_sem.at[d],
            device_id=(b, q), device_id_type=MESH).wait_recv()

    rf[...] = recv[...].astype(jnp.float32).reshape(count * 2 * parts, columns)

    def rows_of(q, k):
        return rf[pl.ds(q * bands * 2 * parts + k, bands, stride=2 * parts), :]

    flipped = lax.broadcasted_iota(jnp.int32, (1, columns), 1)
    scale = 1.0 / (spec * quarters)
    for c in range(CH_DEV):
        blocks = []
        for r in range(2):
            for q in range(quarters):
                full = rows_of(q, 2 * c + r)
                if q + 1 < quarters:
                    full = full + rows_of(q + 1, parts + 2 * c + r)
                blocks.append(full.astype(jnp.bfloat16).astype(jnp.float32))
        bands_of = []
        for s in range(ants * pols):
            turned = None
            for at, block in enumerate(blocks):
                by = (spec * (at - s)) % columns
                moved = pltpu.roll(block, by, 1) if by else block
                turned = moved if turned is None else jnp.where(lane // spec == at, moved, turned)
            bands_of.append(turned)
        got = jnp.concatenate(bands_of, axis=0).astype(jnp.bfloat16)
        right = jnp.dot(all_rows, got, preferred_element_type=jnp.float32).astype(jnp.bfloat16)
        left = jnp.dot(own_rows, got, preferred_element_type=jnp.float32)
        other = pltpu.roll(left, columns // 2, 1)
        other = jnp.where(flipped < columns // 2, other, -other).astype(jnp.bfloat16)
        for o, side in enumerate((left.astype(jnp.bfloat16), other)):
            product = lax.dot_general(side, right, (((1,), (1,)), ((), ())), preferred_element_type=jnp.float32)
            out_ref[o, c] = (product * scale).astype(jnp.bfloat16)


def shards(table, bands, quarters, voltages, flagged, lookup):
    ants, pols, samples = voltages.shape
    spec = samples // FRAME
    steps = FRAME // LANES
    rows = ants * spec
    columns = pols * rows
    x = voltages.reshape(ants, pols, samples // LANES, LANES).transpose(0, 2, 1, 3).reshape(rows, steps * pols, LANES)
    signals = bands * ants * pols
    parts = 2 * CH_DEV
    count = bands * quarters
    group = TAPS * parts * bands
    room = 2 * table.size + 8 * columns * FRAME + 24 * count * parts * columns + 16 * 1024 * 1024
    return pl.pallas_call(
        functools.partial(kernel, bands, quarters, ants, pols, spec),
        out_shape=jax.ShapeDtypeStruct((2, CH_DEV, signals // quarters, signals), jnp.bfloat16),
        in_specs=[
            pl.BlockSpec(memory_space=pltpu.HBM),
            pl.BlockSpec(memory_space=pltpu.HBM),
            pl.BlockSpec(memory_space=pltpu.HBM),
            pl.BlockSpec(memory_space=pltpu.HBM),
        ],
        out_specs=pl.BlockSpec(memory_space=pltpu.VMEM),
        scratch_shapes=[
            pltpu.SMEM((ants,), jnp.int32),
            pltpu.VMEM((1, bands * ants), jnp.int32),
            pltpu.VMEM((CHUNKS, rows, steps * pols // CHUNKS, LANES), jnp.bfloat16),
            pltpu.VMEM((CHUNKS, group, FRAME // CHUNKS), jnp.bfloat16),
            pltpu.VMEM((rows * (steps * pols // CHUNKS + 8), LANES), jnp.float32),
            pltpu.VMEM((bands * 2 * parts, columns), jnp.float32),
            pltpu.VMEM((bands, 2 * parts, columns), jnp.bfloat16),
            pltpu.VMEM((count, 2 * parts, columns), jnp.bfloat16),
            pltpu.VMEM((count * 2 * parts, columns), jnp.float32),
            pltpu.SemaphoreType.DMA((CHUNKS,)),
            pltpu.SemaphoreType.DMA((CHUNKS,)),
            pltpu.SemaphoreType.DMA,
            pltpu.SemaphoreType.DMA,
            pltpu.SemaphoreType.DMA,
            pltpu.SemaphoreType.DMA((count,)),
            pltpu.SemaphoreType.DMA((count,)),
        ],
        compiler_params=pltpu.CompilerParams(
            collective_id=0, has_side_effects=True, vmem_limit_bytes=min(room, 63 * 1024 * 1024)),
    )(*[pltpu.with_memory_space_constraint(v, pltpu.HBM) for v in (flagged, lookup.reshape(1, -1), x, jnp.asarray(table))])


def solution(mesh):
    bands, quarters = mesh.shape["band"], mesh.shape["quarter"]
    return jax.shard_map(
        functools.partial(shards, weights(bands), bands, quarters),
        mesh=mesh,
        in_specs=(P("band", None, "quarter"), P("band"), P()),
        out_specs=P(None, "band", "quarter", None),
        check_vma=False,
    )
```
